32 devices in a mesh: slab: 2 (over x), coarse: 8 (over z, y), fine: 2 (over core).
Axes of the slice: x: 2, y: 2, z: 4, core: 2. Of those that a mesh axis runs over, the one named last changes fastest.
Arguments:
- features: bfloat16 [196608, 256], P(('slab', 'coarse', 'fine')), parts along dimension 0, may hold values from -6 to 6
- weight: bfloat16 [256, 256], replicated, may hold values from -1.5 to 1.5
- bias_vector: float32 [256], replicated, may hold values from -3 to 3
- tile_nbrs: int32 [4, 1536], P(None, ('slab', 'coarse', 'fine')), parts along dimension 1, may hold values from 0 to 767, as said below
- nbr_local: int32 [16, 196608], P(None, ('slab', 'coarse', 'fine')), parts along dimension 1, may hold values from 0 to 511
- edge_count: int32 [16, 196608], P(None, ('slab', 'coarse', 'fine')), parts along dimension 1, may hold values from 1 to 3
- cotangent: bfloat16 [196608, 256], P(('slab', 'coarse', 'fine')), parts along dimension 0, may hold values from -6 to 6
Outputs:
- output: bfloat16 [196608, 256], P(('slab', 'coarse', 'fine')), parts along dimension 0
- grad_features: bfloat16 [196608, 256], P(('slab', 'coarse', 'fine')), parts along dimension 0
- grad_weight: float32 [512, 256], P('slab'), parts along dimension 0
- grad_bias: float32 [512], P('slab'), parts along dimension 0
The draws below stay inside these ranges and needn't reach their ends.
There are 2 independent parts, one for each index of `slab`. The reference program is written for one: setup_inputs(seed, part) draws one part's arguments, and reference() takes and returns one part's arrays. A program takes and returns all parts, laid end to end along the dimension named above; an argument that names none is the same for every part. Nothing has to cross between parts.
Inputs may be any that keep to these rules, and one draw needn't show every extreme that they name: tile_nbrs[0, t] == t for every tile. For each device's tiles (aligned blocks of 48 tiles, owner of tile id u is u // 48), the slots 1 to 3 name tiles of any one other device at most 4 times, and exactly 4 times for at least one other device in every draw.
All inputs are finite; a program needn't handle non-finite values.
Results may differ from the reference program's by a relative error of at most 0.0069.
Values may be sent and summed in bfloat16 or wider, within the bound.
No kernel may reach another device: no remote copies, remote signals or barrier semaphores. Data moves between devices by JAX's collectives and lax.ppermute only.
A program may use at most 192 MiB of HBM per device.

```python
import math
import jax
import jax.numpy as jnp
from jax import lax

C = 256
K = 16
TILE = 128
NB = 4
TD = 48
DEVS = 16
CAP = 4
TILES = 768
POINTS = 98304


def draw_tile_nbrs(key, part):
    keys = jax.random.split(key, 4)
    slot_total = (NB - 1) * TD
    others = DEVS - 1
    counts = jax.random.randint(keys[0], (DEVS, others), 0, CAP + 1)
    forced = jax.random.randint(keys[1], (DEVS,), 0, others)
    counts = jnp.where(jnp.arange(others)[None, :] == forced[:, None], CAP, counts)
    ends = jnp.cumsum(counts, axis=1)
    starts = ends - counts
    orders = jax.vmap(lambda single: jax.random.permutation(single, slot_total))(jax.random.split(keys[2], DEVS))
    inside = (orders[:, :, None] >= starts[:, None, :]) & (orders[:, :, None] < ends[:, None, :])
    offsets = jnp.sum(inside.astype(jnp.int32) * (jnp.arange(others) + 1)[None, None, :], axis=2)
    owners = (jnp.arange(DEVS)[:, None] + offsets) % DEVS
    within = jax.random.randint(keys[3], (DEVS, slot_total), 0, TD)
    linked = (owners * TD + within).reshape(DEVS, TD, NB - 1)
    itself = (jnp.arange(DEVS)[:, None] * TD + jnp.arange(TD)[None, :])[:, :, None]
    full_table = jnp.concatenate([itself, linked], axis=2).reshape(DEVS * TD, NB)
    return full_table.T.astype(jnp.int32)


def set_ends(result, rng, least, largest):
    shape = result.shape
    place = [jax.random.randint(jax.random.fold_in(rng, axis), (), 0, shape[axis]) for axis in range(len(shape))]
    result = result.at[tuple(place)].set(least)
    longest = shape.index(max(shape))
    place[longest] = (place[longest] + 1) % shape[longest]
    return result.at[tuple(place)].set(largest)


def levels(rng, dims, cuts, smallest, largest):
    def one(dim, shards_of):
        heights = jax.random.uniform(jax.random.fold_in(jax.random.fold_in(rng, 6), dim), (shards_of,), jnp.float32, smallest / len(cuts), largest / len(cuts))
        return jnp.repeat(jnp.exp(heights), dims[dim] // shards_of).reshape((-1,) + (1,) * (len(dims) - dim - 1))

    gain = one(*cuts[0])
    for cut in cuts[1:]:
        gain = gain * one(*cut)
    return gain


def noise(key, shape, spread, most, pieces=(), kind=jnp.bfloat16):
    values = jax.random.normal(key, shape, jnp.float32) * spread
    if len(pieces) > 0:
        values = levels(key, shape, pieces, -0.22, 0.18) * values
    return jnp.clip(values, min=-most, max=most).astype(kind)


def setup_inputs(seed: int = 0, part: int = 0) -> dict:
    key_list = jax.random.split(jax.random.key(seed), 8)
    part_keys = jax.random.split(jax.random.fold_in(key_list[7], part), 8)
    features = noise(part_keys[0], (POINTS, C), 1.0, 6.0, ((0, 16),))
    weight = noise(key_list[1], (C, C), (C // 16) ** -0.5, 1.5)
    bias_vector = noise(key_list[2], (C,), 0.5, 3.0, (), jnp.float32)
    tile_nbrs = draw_tile_nbrs(jax.random.fold_in(jax.random.fold_in(key_list[7], part), 71), part)
    nbr_local = set_ends(jax.random.randint(part_keys[4], (K, POINTS), 0, NB * TILE), jax.random.fold_in(part_keys[4], 1), 0, (NB * TILE) - 1).astype(jnp.int32)
    edge_count = set_ends(jax.random.randint(part_keys[5], (K, POINTS), 1, 4), jax.random.fold_in(part_keys[5], 1), 1, 3).astype(jnp.int32)
    cotangent = noise(part_keys[6], (POINTS, C), 1.0, 6.0, ((0, 16),))
    return {"features": features, "weight": weight, "bias_vector": bias_vector, "tile_nbrs": tile_nbrs, "nbr_local": nbr_local, "edge_count": edge_count, "cotangent": cotangent}


def group_blocks(nbr_part, count_part):
    point_count = nbr_part.shape[1]
    degree = lax.optimization_barrier(jnp.sum(count_part.astype(jnp.float32), axis=0))
    weights = count_part.astype(jnp.float32) / degree[None, :]
    points = jnp.broadcast_to(jnp.arange(point_count, dtype=jnp.int32)[None, :], nbr_part.shape)
    dense_rows = jnp.zeros((point_count, NB * TILE), jnp.float32).at[points, nbr_part].add(weights)
    return dense_rows.astype(jnp.bfloat16).reshape(point_count // TILE, TILE, NB * TILE)

def reference(features, weight, bias_vector, tile_nbrs, nbr_local, edge_count, cotangent):
    x_tiles = features.reshape(TILES, TILE, C)

    def group_parts(group_index):
        first_tile = (group_index * TD).astype(jnp.int32)
        tile_rows = lax.dynamic_slice_in_dim(tile_nbrs, first_tile, TD, 1)
        nbr_part = lax.dynamic_slice_in_dim(nbr_local, first_tile * TILE, TD * TILE, 1)
        count_part = lax.dynamic_slice_in_dim(edge_count, first_tile * TILE, TD * TILE, 1)
        return (tile_rows, group_blocks(nbr_part, count_part))

    def forward_group(group_index):
        tile_rows, blocks = group_parts(group_index)
        nearby = x_tiles[tile_rows.T].reshape(TD, NB * TILE, C)
        aggregated = jnp.einsum('tij,tjc->tic', blocks.astype(jnp.float32), nearby.astype(jnp.float32))
        return aggregated.astype(jnp.bfloat16).reshape(TD * TILE, C)
    group_ids = jnp.arange(DEVS, dtype=jnp.int32)
    aggregated = lax.map(forward_group, group_ids).reshape(POINTS, C)
    preact = jnp.dot(aggregated, weight, preferred_element_type=jnp.float32) + bias_vector
    sigma = jax.nn.sigmoid(preact)
    output = (preact * sigma).astype(jnp.bfloat16)
    slope = sigma * (1.0 + preact * (1.0 - sigma))
    preact_grad = (cotangent.astype(jnp.float32) * slope).astype(jnp.bfloat16)
    normalizer = 1.0 / math.sqrt(POINTS)
    grad_weight = jnp.dot(aggregated.T, preact_grad, preferred_element_type=jnp.float32) * normalizer
    grad_bias = lax.optimization_barrier(jnp.sum(preact_grad.astype(jnp.float32), axis=0)) * normalizer
    gradient = jnp.dot(preact_grad, weight.T, preferred_element_type=jnp.float32).astype(jnp.bfloat16)
    gradient = gradient.reshape(TILES, TILE, C)

    def backward_group(summed, group_index):
        tile_rows, blocks = group_parts(group_index)
        grad_part = lax.dynamic_slice_in_dim(gradient, (group_index * TD).astype(jnp.int32), TD, 0)
        backward = jnp.einsum('tij,tic->tjc', blocks.astype(jnp.float32), grad_part.astype(jnp.float32))
        backward = backward.reshape(TD, NB, TILE, C)
        return (summed.at[tile_rows.T].add(backward), None)
    summed, unused = lax.scan(backward_group, jnp.zeros((TILES, TILE, C), jnp.float32), group_ids)
    grad_features = summed.reshape(POINTS, C).astype(jnp.bfloat16)
    return (output, grad_features, grad_weight, grad_bias)
```

```python
import math

import jax
import jax.numpy as jnp
from jax import lax
from jax.experimental import pallas as pl
from jax.experimental.pallas import tpu as pltpu
from jax.sharding import PartitionSpec as P

C = 256
TILE = 128
NB = 4
GROUP = ("coarse", "fine")
VMEM = pltpu.MemorySpace.VMEM
SMEM = pltpu.MemorySpace.SMEM


def whole(space=VMEM):
    return pl.BlockSpec(memory_space=space)


def pack_kernel(position_ref, table_ref, x_ref, packed_ref, wanted_ref, wanted_s, table_sem, sems):
    devices, slot_count = table_ref.shape
    tile_count = x_ref.shape[0]
    capacity = packed_ref.shape[0] // devices
    position = position_ref[0]
    within = table_ref[...] - position * tile_count
    asker = lax.broadcasted_iota(jnp.int32, within.shape, 0)
    mine = (within >= 0) & (within < tile_count) & (asker != position)
    ones = jnp.where(mine, 1.0, 0.0)
    earlier = lax.broadcasted_iota(jnp.int32, (slot_count, slot_count), 0)
    later = lax.broadcasted_iota(jnp.int32, (slot_count, slot_count), 1)
    before = jnp.where(earlier < later, 1.0, 0.0).astype(jnp.bfloat16)
    ranking = jnp.dot(ones.astype(jnp.bfloat16), before, preferred_element_type=jnp.float32)
    lane = lax.broadcasted_iota(jnp.int32, wanted_ref.shape, 1)
    wanted = jnp.full(wanted_ref.shape, -1, jnp.int32)
    for rank in range(capacity):
        chosen = jnp.where(mine & (ranking.astype(jnp.int32) == rank), within + 1, 0)
        found = jnp.sum(chosen.astype(jnp.float32), axis=1, keepdims=True).astype(jnp.int32) - 1
        wanted = jnp.where(lane == rank, found, wanted)
    wanted_ref[...] = wanted
    copy = pltpu.make_async_copy(wanted_ref, wanted_s, table_sem)
    copy.start()
    copy.wait()
    for device in range(devices):
        for rank in range(capacity):
            tile = wanted_s[device, rank]

            @pl.when(tile >= 0)
            def _():
                slot = device * capacity + rank
                pltpu.make_async_copy(x_ref.at[tile], packed_ref.at[slot], sems.at[slot]).start()

    for device in range(devices):
        for rank in range(capacity):
            tile = wanted_s[device, rank]

            @pl.when(tile >= 0)
            def _():
                slot = device * capacity + rank
                pltpu.make_async_copy(x_ref.at[tile], packed_ref.at[slot], sems.at[slot]).wait()


def pack(position, table, x_tiles, capacity):
    devices = table.shape[0]
    return pl.pallas_call(
        pack_kernel,
        name="pack",
        in_specs=[whole(SMEM), whole(), whole()],
        out_specs=[pl.BlockSpec(memory_space=pl.ANY), whole()],
        out_shape=[
            jax.ShapeDtypeStruct((devices * capacity, TILE, C), jnp.bfloat16),
            jax.ShapeDtypeStruct((devices, 128), jnp.int32),
        ],
        scratch_shapes=[
            pltpu.SMEM((devices, 128), jnp.int32),
            pltpu.SemaphoreType.DMA,
            pltpu.SemaphoreType.DMA((devices * capacity,)),
        ],
        compiler_params=pltpu.CompilerParams(vmem_limit_bytes=16 << 20),
    )(position, table, x_tiles)


def blocks_kernel(nbr_ref, count_ref, rows_ref, columns_ref):
    counts = count_ref[...].astype(jnp.float32)
    weights = counts / jnp.sum(counts, axis=0, keepdims=True)
    targets = nbr_ref[...]
    for slot in range(NB):
        local = lax.broadcasted_iota(jnp.int32, (TILE, TILE), 0) + slot * TILE
        total = jnp.zeros((TILE, TILE), jnp.float32)
        for k in range(targets.shape[0]):
            total += jnp.where(targets[k : k + 1] == local, weights[k : k + 1], 0.0)
        columns_ref[0, slot] = total.astype(jnp.bfloat16)
        rows_ref[0, :, slot * TILE : (slot + 1) * TILE] = total.T.astype(jnp.bfloat16)


def build_blocks(nbr, count):
    entries, points = nbr.shape
    tile_count = points // TILE
    return pl.pallas_call(
        blocks_kernel,
        name="blocks",
        grid=(tile_count,),
        in_specs=[pl.BlockSpec((entries, TILE), lambda t: (0, t))] * 2,
        out_specs=[
            pl.BlockSpec((1, TILE, NB * TILE), lambda t: (t, 0, 0)),
            pl.BlockSpec((1, NB, TILE, TILE), lambda t: (t, 0, 0, 0)),
        ],
        out_shape=[
            jax.ShapeDtypeStruct((tile_count, TILE, NB * TILE), jnp.bfloat16),
            jax.ShapeDtypeStruct((tile_count, NB, TILE, TILE), jnp.bfloat16),
        ],
        compiler_params=pltpu.CompilerParams(vmem_limit_bytes=8 << 20),
    )(nbr, count)


def middle_kernel(
    rows_index, term_tile, term_slot, rows_ref, columns_ref, x_ref, arrived_ref, weight_ref, bias_ref, cot_ref,
    out_ref, agg_ref, pg_ref, grad_ref, terms_ref, near, terms, near_sems, sems,
):
    tile_count = x_ref.shape[0]
    slots = arrived_ref.shape[0]
    own = pltpu.make_async_copy(x_ref, near.at[pl.ds(0, tile_count)], near_sems.at[0])
    others = pltpu.make_async_copy(arrived_ref, near.at[pl.ds(tile_count, slots)], near_sems.at[1])
    own.start()
    others.start()
    own.wait()
    others.wait()
    weight = weight_ref[...]
    bias = bias_ref[...]

    def tile_step(t, carry):
        rows = rows_ref[t]
        first = jnp.concatenate([near[t], near[rows_index[1, t]]], axis=0)
        second = jnp.concatenate([near[rows_index[2, t]], near[rows_index[3, t]]], axis=0)
        total = jnp.dot(rows[:, : 2 * TILE], first, preferred_element_type=jnp.float32)
        total += jnp.dot(rows[:, 2 * TILE :], second, preferred_element_type=jnp.float32)
        aggregated = total.astype(jnp.bfloat16)
        agg_ref[t] = aggregated
        preact = jnp.dot(aggregated, weight, preferred_element_type=jnp.float32) + bias
        sigma = jax.nn.sigmoid(preact)
        out_ref[t] = (preact * sigma).astype(jnp.bfloat16)
        slope = sigma * (1.0 + preact * (1.0 - sigma))
        preact_grad = (cot_ref[t].astype(jnp.float32) * slope).astype(jnp.bfloat16)
        pg_ref[t] = preact_grad
        grad_ref[t] = lax.dot_general(
            preact_grad, weight, (((1,), (1,)), ((), ())), preferred_element_type=jnp.float32
        ).astype(jnp.bfloat16)
        return carry

    lax.fori_loop(0, tile_count, tile_step, 0)

    per = slots // sems.shape[0]

    def term_step(device, carry):
        for rank in range(per):
            slot = device * per + rank
            t = term_tile[slot]
            terms[slot] = jnp.dot(
                columns_ref[t, term_slot[slot]], grad_ref[t], preferred_element_type=jnp.float32
            ).astype(jnp.bfloat16)
        part = pl.ds(device * per, per)
        pltpu.make_async_copy(terms.at[part], terms_ref.at[part], sems.at[device]).start()
        return carry

    lax.fori_loop(0, sems.shape[0], term_step, 0)

    def finish(device, carry):
        part = pl.ds(device * per, per)
        pltpu.make_async_copy(terms.at[part], terms_ref.at[part], sems.at[device]).wait()
        return carry

    lax.fori_loop(0, sems.shape[0], finish, 0)


def middle(rows_index, term_tile, term_slot, rows, columns, x_tiles, arrived, weight, bias, cot, devices):
    tile_count = x_tiles.shape[0]
    slots = arrived.shape[0]
    tiles = jax.ShapeDtypeStruct((tile_count, TILE, C), jnp.bfloat16)
    return pl.pallas_call(
        middle_kernel,
        name="middle",
        in_specs=[whole(SMEM)] * 3 + [whole()] * 3 + [pl.BlockSpec(memory_space=pl.ANY)] + [whole()] * 3,
        out_specs=[whole()] * 4 + [pl.BlockSpec(memory_space=pl.ANY)],
        out_shape=[tiles] * 4 + [jax.ShapeDtypeStruct((slots, TILE, C), jnp.bfloat16)],
        scratch_shapes=[
            pltpu.VMEM((tile_count + slots, TILE, C), jnp.bfloat16),
            pltpu.VMEM((slots, TILE, C), jnp.bfloat16),
            pltpu.SemaphoreType.DMA((2,)),
            pltpu.SemaphoreType.DMA((devices,)),
        ],
        compiler_params=pltpu.CompilerParams(vmem_limit_bytes=58 << 20),
    )(rows_index, term_tile, term_slot, rows, columns, x_tiles, arrived, weight, bias, cot)


def local_kernel(target_ref, columns_ref, grad_ref, total_ref):
    tile_count = grad_ref.shape[0]

    def own_step(t, carry):
        total_ref[t] = jnp.dot(columns_ref[t, 0], grad_ref[t], preferred_element_type=jnp.float32)
        return carry

    lax.fori_loop(0, tile_count, own_step, 0)

    def other_step(t, carry):
        for slot in range(1, NB):
            target = target_ref[slot, t]

            @pl.when(target < tile_count)
            def _():
                total_ref[target] += jnp.dot(
                    columns_ref[t, slot], grad_ref[t], preferred_element_type=jnp.float32
                )

        return carry

    lax.fori_loop(0, tile_count, other_step, 0)


def local_terms(rows_index, columns, grad):
    return pl.pallas_call(
        local_kernel,
        name="local_terms",
        in_specs=[whole(SMEM), whole(), whole()],
        out_specs=whole(),
        out_shape=jax.ShapeDtypeStruct(grad.shape, jnp.float32),
        compiler_params=pltpu.CompilerParams(vmem_limit_bytes=24 << 20),
    )(rows_index, columns, grad)


def final_kernel(wanted_ref, local_ref, returned_ref, out_ref, total, returned, total_sem, sems):
    tile_count = local_ref.shape[0]
    devices = sems.shape[0]
    per = returned_ref.shape[0] // devices
    first = pltpu.make_async_copy(local_ref, total, total_sem)
    first.start()
    copies = []
    for device in range(devices):
        part = pl.ds(device * per, per)
        copies.append(pltpu.make_async_copy(returned_ref.at[part], returned.at[part], sems.at[device]))
        copies[-1].start()
    first.wait()
    for device in range(devices):
        copies[device].wait()
        for rank in range(per):
            target = wanted_ref[device, rank]

            @pl.when(target >= 0)
            def _():
                total[target] += returned[device * per + rank].astype(jnp.float32)

    def round_step(t, carry):
        out_ref[t] = total[t].astype(jnp.bfloat16)
        return carry

    lax.fori_loop(0, tile_count, round_step, 0)


def final_sum(wanted, local, returned, devices):
    return pl.pallas_call(
        final_kernel,
        name="final_sum",
        in_specs=[whole(SMEM), pl.BlockSpec(memory_space=pl.ANY), pl.BlockSpec(memory_space=pl.ANY)],
        out_specs=whole(),
        out_shape=jax.ShapeDtypeStruct(local.shape, jnp.bfloat16),
        scratch_shapes=[
            pltpu.VMEM(local.shape, jnp.float32),
            pltpu.VMEM(returned.shape, jnp.bfloat16),
            pltpu.SemaphoreType.DMA,
            pltpu.SemaphoreType.DMA((devices,)),
        ],
        compiler_params=pltpu.CompilerParams(vmem_limit_bytes=24 << 20),
    )(wanted, local, returned)


def exchange(array, devices):
    parted = array.reshape((devices, array.shape[0] // devices) + array.shape[1:])
    return lax.all_to_all(parted, GROUP, split_axis=0, concat_axis=0, tiled=True).reshape(array.shape)


def group_sum(part, devices, position):
    bits = devices.bit_length() - 1
    for bit in range(bits):
        half = part.shape[0] // 2
        upper = (position >> bit) & 1 == 1
        pairs = [(d, d ^ (1 << bit)) for d in range(devices)]
        sent = jnp.where(upper, part[:half], part[half:])
        kept = jnp.where(upper, part[half:], part[:half])
        part = kept + lax.ppermute(sent, GROUP, pairs)
    for bit in reversed(range(bits)):
        upper = (position >> bit) & 1 == 1
        pairs = [(d, d ^ (1 << bit)) for d in range(devices)]
        other = lax.ppermute(part, GROUP, pairs)
        part = jnp.where(upper, jnp.concatenate([other, part]), jnp.concatenate([part, other]))
    return part


def shards(features, weight, bias_vector, tile_nbrs, nbr_local, edge_count, cotangent):
    devices = lax.axis_size("coarse") * lax.axis_size("fine")
    position = lax.axis_index(GROUP)
    tile_count = features.shape[0] // TILE
    capacity = max(1, (NB - 1) * tile_count // (2 * (devices - 1)))
    slots = devices * capacity
    x_tiles = features.reshape(tile_count, TILE, C)
    cot_tiles = cotangent.reshape(tile_count, TILE, C)

    table = lax.all_to_all(
        jnp.broadcast_to(tile_nbrs.reshape(1, -1), (devices, NB * tile_count)),
        GROUP,
        split_axis=0,
        concat_axis=0,
        tiled=True,
    )
    packed, wanted = pack(position.reshape(1).astype(jnp.int32), table, x_tiles, capacity)
    arrived = exchange(packed, devices)

    nbr_local, edge_count, tile_nbrs, packed = lax.optimization_barrier(
        (nbr_local, edge_count, tile_nbrs, packed)
    )
    rows, columns = build_blocks(nbr_local, edge_count)
    owners = tile_nbrs // tile_count
    within = tile_nbrs % tile_count
    remote = owners != position
    onehot = (
        (owners.reshape(-1)[:, None] == jnp.arange(devices, dtype=jnp.int32)[None, :])
        & remote.reshape(-1)[:, None]
    ).astype(jnp.int32)
    ranking = jnp.sum((jnp.cumsum(onehot, axis=0) - onehot) * onehot, axis=1).reshape(owners.shape)
    buffer_slot = jnp.where(remote, owners * capacity + ranking, slots)
    rows_index = jnp.where(remote, tile_count + buffer_slot, within)
    held = (buffer_slot.reshape(-1)[None, :] == jnp.arange(slots, dtype=jnp.int32)[:, None]).astype(jnp.int32)
    source = jnp.sum(held * jnp.arange(NB * tile_count, dtype=jnp.int32)[None, :], axis=1)
    term_tile = source % tile_count
    term_slot = source // tile_count

    out, aggregated, preact_grad, gradient, terms = middle(
        rows_index, term_tile, term_slot, rows, columns, x_tiles, arrived, weight,
        bias_vector.reshape(1, C), cot_tiles, devices,
    )
    returned = exchange(terms, devices)
    aggregated, preact_grad, gradient, terms = lax.optimization_barrier(
        (aggregated, preact_grad, gradient, terms)
    )
    preact_grad = preact_grad.reshape(-1, C)
    weight_part = lax.dot_general(
        aggregated.reshape(-1, C), preact_grad, (((0,), (0,)), ((), ())), preferred_element_type=jnp.float32
    )
    bias_part = jnp.sum(preact_grad.astype(jnp.float32), axis=0)
    part = jnp.concatenate([weight_part, jnp.broadcast_to(bias_part[None], (C // 2, C))])
    summed = group_sum(part, devices, position)
    normalizer = 1.0 / math.sqrt(features.shape[0] * devices)
    summed = summed * normalizer
    local = local_terms(rows_index, columns, gradient)
    grad_features = final_sum(wanted, local, returned, devices)
    return (out.reshape(-1, C), grad_features.reshape(-1, C), summed[:C], summed[C])


def solution(mesh):
    return jax.shard_map(
        shards,
        mesh=mesh,
        in_specs=(
            P(("slab", "coarse", "fine"), None),
            P(),
            P(),
            P(None, ("slab", "coarse", "fine")),
            P(None, ("slab", "coarse", "fine")),
            P(None, ("slab", "coarse", "fine")),
            P(("slab", "coarse", "fine"), None),
        ),
        out_specs=(
            P(("slab", "coarse", "fine"), None),
            P(("slab", "coarse", "fine"), None),
            P("slab", None),
            P("slab"),
        ),
        check_vma=False,
    )
```

```python
import math

import jax
import jax.numpy as jnp
from jax import lax
from jax.experimental import pallas as pl
from jax.experimental.pallas import tpu as pltpu
from jax.sharding import PartitionSpec as P

C = 256
TILE = 128
NB = 4
GROUP = ("coarse", "fine")
VMEM = pltpu.MemorySpace.VMEM
SMEM = pltpu.MemorySpace.SMEM
HBM = pltpu.MemorySpace.HBM
PIECE = 32
MIDDLE_VMEM = 20 << 20


def whole(space=VMEM):
    return pl.BlockSpec(memory_space=space)


def pack_kernel(position_ref, table_ref, x_ref, packed_ref, wanted_ref, x_held, wanted_s, x_sem, table_sem, sems):
    devices, slot_count = table_ref.shape
    tile_count = x_ref.shape[0]
    capacity = packed_ref.shape[0] // devices
    load = pltpu.make_async_copy(x_ref, x_held, x_sem)
    load.start()
    position = position_ref[0]
    within = table_ref[...] - position * tile_count
    asker = lax.broadcasted_iota(jnp.int32, within.shape, 0)
    mine = (within >= 0) & (within < tile_count) & (asker != position)
    ones = jnp.where(mine, 1.0, 0.0)
    earlier = lax.broadcasted_iota(jnp.int32, (slot_count, slot_count), 0)
    later = lax.broadcasted_iota(jnp.int32, (slot_count, slot_count), 1)
    before = jnp.where(earlier < later, 1.0, 0.0).astype(jnp.bfloat16)
    ranking = jnp.dot(ones.astype(jnp.bfloat16), before, preferred_element_type=jnp.float32)
    lane = lax.broadcasted_iota(jnp.int32, wanted_ref.shape, 1)
    wanted = jnp.full(wanted_ref.shape, -1, jnp.int32)
    for rank in range(capacity):
        chosen = jnp.where(mine & (ranking.astype(jnp.int32) == rank), within + 1, 0)
        found = jnp.sum(chosen.astype(jnp.float32), axis=1, keepdims=True).astype(jnp.int32) - 1
        wanted = jnp.where(lane == rank, found, wanted)
    wanted_ref[...] = wanted
    copy = pltpu.make_async_copy(wanted_ref, wanted_s, table_sem)
    copy.start()
    copy.wait()
    load.wait()

    def each(act):
        def step(device, carry):
            for rank in range(capacity):
                tile = wanted_s[device, rank]

                @pl.when(tile >= 0)
                def _():
                    slot = device * capacity + rank
                    act(pltpu.make_async_copy(x_held.at[tile], packed_ref.at[slot], sems.at[slot]))

            return carry

        lax.fori_loop(0, devices, step, 0)

    each(lambda copy: copy.start())
    each(lambda copy: copy.wait())


def pack(position, table, x_tiles, capacity):
    devices = table.shape[0]
    return pl.pallas_call(
        pack_kernel,
        name="pack",
        in_specs=[whole(SMEM), whole(), whole(HBM)],
        out_specs=[whole(HBM), whole()],
        out_shape=[
            jax.ShapeDtypeStruct((devices * capacity, TILE, C), jnp.bfloat16),
            jax.ShapeDtypeStruct((devices, 128), jnp.int32),
        ],
        scratch_shapes=[
            pltpu.VMEM(x_tiles.shape, jnp.bfloat16),
            pltpu.SMEM((devices, 128), jnp.int32),
            pltpu.SemaphoreType.DMA,
            pltpu.SemaphoreType.DMA,
            pltpu.SemaphoreType.DMA((devices * capacity,)),
        ],
        compiler_params=pltpu.CompilerParams(vmem_limit_bytes=16 << 20),
    )(position, table, x_tiles)


def blocks_kernel(nbr_ref, count_ref, rows_ref, columns_ref):
    counts = count_ref[...].astype(jnp.float32)
    weights = counts / jnp.sum(counts, axis=0, keepdims=True)
    targets = nbr_ref[...]
    for slot in range(NB):
        local = lax.broadcasted_iota(jnp.int32, (TILE, TILE), 0) + slot * TILE
        total = jnp.zeros((TILE, TILE), jnp.float32)
        for k in range(targets.shape[0]):
            total += jnp.where(targets[k : k + 1] == local, weights[k : k + 1], 0.0)
        columns_ref[0, slot] = total.astype(jnp.bfloat16)
        rows_ref[0, :, slot * TILE : (slot + 1) * TILE] = total.T.astype(jnp.bfloat16)


def build_blocks(nbr, count):
    entries, points = nbr.shape
    tile_count = points // TILE
    return pl.pallas_call(
        blocks_kernel,
        name="blocks",
        grid=(tile_count,),
        in_specs=[pl.BlockSpec((entries, TILE), lambda t: (0, t))] * 2,
        out_specs=[
            pl.BlockSpec((1, TILE, NB * TILE), lambda t: (t, 0, 0)),
            pl.BlockSpec((1, NB, TILE, TILE), lambda t: (t, 0, 0, 0)),
        ],
        out_shape=[
            jax.ShapeDtypeStruct((tile_count, TILE, NB * TILE), jnp.bfloat16),
            jax.ShapeDtypeStruct((tile_count, NB, TILE, TILE), jnp.bfloat16),
        ],
        compiler_params=pltpu.CompilerParams(vmem_limit_bytes=8 << 20),
    )(nbr, count)


def middle_kernel(
    rows_index, term_tile, rows_ref, sent_ref, x_ref, arrived_ref, weight_ref, bias_ref, cot_ref,
    out_ref, agg_ref, pg_ref, grad_ref, terms_ref, near, terms, pre, near_sems, sems,
):
    tile_count = x_ref.shape[0]
    slots = arrived_ref.shape[0]
    group = pre.shape[0] // TILE
    others = pltpu.make_async_copy(arrived_ref, near.at[pl.ds(tile_count, slots)], near_sems.at[1])
    others.start()
    own = pltpu.make_async_copy(x_ref, near.at[pl.ds(0, tile_count)], near_sems.at[0])
    own.start()
    own.wait()
    others.wait()
    weight = weight_ref[...]
    bias = bias_ref[...]

    def group_step(step, carry):
        start = step * group
        for at in range(group):
            t = start + at
            rows = rows_ref[t]
            first = jnp.concatenate([near[t], near[rows_index[1, t]]], axis=0)
            second = jnp.concatenate([near[rows_index[2, t]], near[rows_index[3, t]]], axis=0)
            total = jnp.dot(rows[:, : 2 * TILE], first, preferred_element_type=jnp.float32)
            total += jnp.dot(rows[:, 2 * TILE :], second, preferred_element_type=jnp.float32)
            agg_ref[t] = total.astype(jnp.bfloat16)
        aggregated = agg_ref[pl.ds(start, group)].reshape(group * TILE, C)
        pre[...] = jnp.dot(aggregated, weight, preferred_element_type=jnp.float32) + bias
        for piece in range(group * TILE // PIECE):
            t = start + piece * PIECE // TILE
            part = pl.ds(piece * PIECE % TILE, PIECE)
            preact = pre[piece * PIECE : (piece + 1) * PIECE]
            sigma = jax.nn.sigmoid(preact)
            out_ref[t, part] = (preact * sigma).astype(jnp.bfloat16)
            slope = sigma * (1.0 + preact * (1.0 - sigma))
            pg_ref[t, part] = (cot_ref[t, part].astype(jnp.float32) * slope).astype(jnp.bfloat16)
        preact_grad = pg_ref[pl.ds(start, group)].reshape(group * TILE, C)
        gradient = lax.dot_general(
            preact_grad, weight, (((1,), (1,)), ((), ())), preferred_element_type=jnp.float32
        )
        grad_ref[pl.ds(start, group)] = gradient.astype(jnp.bfloat16).reshape(group, TILE, C)
        return carry

    lax.fori_loop(0, tile_count // group, group_step, 0)

    per = slots // sems.shape[0]

    def term_step(device, carry):
        for rank in range(per):
            slot = device * per + rank
            terms[slot] = jnp.dot(
                sent_ref[slot], grad_ref[term_tile[slot]], preferred_element_type=jnp.float32
            ).astype(jnp.bfloat16)
        part = pl.ds(device * per, per)
        pltpu.make_async_copy(terms.at[part], terms_ref.at[part], sems.at[device]).start()
        return carry

    lax.fori_loop(0, sems.shape[0], term_step, 0)

    def finish(device, carry):
        part = pl.ds(device * per, per)
        pltpu.make_async_copy(terms.at[part], terms_ref.at[part], sems.at[device]).wait()
        return carry

    lax.fori_loop(0, sems.shape[0], finish, 0)


def middle(rows_index, term_tile, rows, sent, x_tiles, arrived, weight, bias, cot, devices):
    tile_count = x_tiles.shape[0]
    slots = arrived.shape[0]
    group = math.gcd(tile_count, 8)
    tiles = jax.ShapeDtypeStruct((tile_count, TILE, C), jnp.bfloat16)
    return pl.pallas_call(
        middle_kernel,
        name="middle",
        in_specs=[whole(SMEM)] * 2 + [whole()] * 3 + [whole(HBM)] + [whole()] * 3,
        out_specs=[whole()] * 4 + [whole(HBM)],
        out_shape=[tiles] * 4 + [jax.ShapeDtypeStruct((slots, TILE, C), jnp.bfloat16)],
        scratch_shapes=[
            pltpu.VMEM((tile_count + slots, TILE, C), jnp.bfloat16),
            pltpu.VMEM((slots, TILE, C), jnp.bfloat16),
            pltpu.VMEM((group * TILE, C), jnp.float32),
            pltpu.SemaphoreType.DMA((2,)),
            pltpu.SemaphoreType.DMA((devices,)),
        ],
        compiler_params=pltpu.CompilerParams(vmem_limit_bytes=MIDDLE_VMEM),
    )(rows_index, term_tile, rows, sent, x_tiles, arrived, weight, bias, cot)


def local_kernel(target_ref, columns_ref, grad_ref, total_ref):
    tile_count = grad_ref.shape[0]

    def own_step(t, carry):
        total_ref[t] = jnp.dot(columns_ref[t, 0], grad_ref[t], preferred_element_type=jnp.float32)
        return carry

    lax.fori_loop(0, tile_count, own_step, 0)

    def other_step(t, carry):
        for slot in range(1, NB):
            target = target_ref[slot, t]

            @pl.when(target < tile_count)
            def _():
                total_ref[target] += jnp.dot(
                    columns_ref[t, slot], grad_ref[t], preferred_element_type=jnp.float32
                )

        return carry

    lax.fori_loop(0, tile_count, other_step, 0)


def local_terms(rows_index, columns, grad):
    return pl.pallas_call(
        local_kernel,
        name="local_terms",
        in_specs=[whole(SMEM), whole(), whole()],
        out_specs=whole(),
        out_shape=jax.ShapeDtypeStruct(grad.shape, jnp.float32),
        compiler_params=pltpu.CompilerParams(vmem_limit_bytes=24 << 20),
    )(rows_index, columns, grad)


def final_kernel(wanted_ref, local_ref, returned_ref, out_ref, total, returned, total_sem, sems):
    tile_count = local_ref.shape[0]
    devices = sems.shape[0]
    per = returned_ref.shape[0] // devices
    first = pltpu.make_async_copy(local_ref, total, total_sem)
    first.start()
    copies = []
    for device in range(devices):
        part = pl.ds(device * per, per)
        copies.append(pltpu.make_async_copy(returned_ref.at[part], returned.at[part], sems.at[device]))
        copies[-1].start()
    first.wait()
    for device in range(devices):
        copies[device].wait()
        for rank in range(per):
            target = wanted_ref[device, rank]

            @pl.when(target >= 0)
            def _():
                total[target] += returned[device * per + rank].astype(jnp.float32)

    def round_step(t, carry):
        out_ref[t] = total[t].astype(jnp.bfloat16)
        return carry

    lax.fori_loop(0, tile_count, round_step, 0)


def final_sum(wanted, local, returned, devices):
    return pl.pallas_call(
        final_kernel,
        name="final_sum",
        in_specs=[whole(SMEM), pl.BlockSpec(memory_space=pl.ANY), pl.BlockSpec(memory_space=pl.ANY)],
        out_specs=whole(),
        out_shape=jax.ShapeDtypeStruct(local.shape, jnp.bfloat16),
        scratch_shapes=[
            pltpu.VMEM(local.shape, jnp.float32),
            pltpu.VMEM(returned.shape, jnp.bfloat16),
            pltpu.SemaphoreType.DMA,
            pltpu.SemaphoreType.DMA((devices,)),
        ],
        compiler_params=pltpu.CompilerParams(vmem_limit_bytes=24 << 20),
    )(wanted, local, returned)


def exchange(array, devices):
    parted = array.reshape((devices, array.shape[0] // devices) + array.shape[1:])
    return lax.all_to_all(parted, GROUP, split_axis=0, concat_axis=0, tiled=True).reshape(array.shape)


def group_sum(part, devices, position, hold):
    bits = devices.bit_length() - 1
    low = bits - 2

    def swap(piece, difference):
        return lax.ppermute(piece, GROUP, [(d, d ^ difference) for d in range(devices)])

    for bit in range(low):
        half = part.shape[0] // 2
        upper = (position >> bit) & 1 == 1
        got = swap(jnp.where(upper, part[:half], part[half:]), 1 << bit)
        kept = jnp.where(upper, part[half:], part[:half])
        if bit == low - 1:
            got = hold(got)
        part = kept + got
    quarters = part.reshape(4, part.shape[0] // 4, C)
    place = position >> low
    got = [swap(lax.dynamic_index_in_dim(quarters, place ^ r, 0, False), r << low) for r in range(1, 4)]
    part = lax.dynamic_index_in_dim(quarters, place, 0, False) + got[0] + got[1] + got[2]
    gathered = jnp.stack([part] + [swap(part, r << low) for r in range(1, 4)])
    part = jnp.concatenate([lax.dynamic_index_in_dim(gathered, place ^ j, 0, False) for j in range(4)])
    for bit in reversed(range(low)):
        upper = (position >> bit) & 1 == 1
        other = swap(part, 1 << bit)
        part = jnp.where(upper, jnp.concatenate([other, part]), jnp.concatenate([part, other]))
    return part


def shards(features, weight, bias_vector, tile_nbrs, nbr_local, edge_count, cotangent):
    devices = lax.axis_size("coarse") * lax.axis_size("fine")
    position = lax.axis_index(GROUP)
    tile_count = features.shape[0] // TILE
    capacity = max(1, (NB - 1) * tile_count // (2 * (devices - 1)))
    slots = devices * capacity
    x_tiles = features.reshape(tile_count, TILE, C)
    cot_tiles = cotangent.reshape(tile_count, TILE, C)

    table = lax.all_to_all(
        jnp.broadcast_to(tile_nbrs.reshape(1, -1), (devices, NB * tile_count)),
        GROUP,
        split_axis=0,
        concat_axis=0,
        tiled=True,
    )
    packed, wanted = pack(position.reshape(1).astype(jnp.int32), table, x_tiles, capacity)
    arrived = exchange(packed, devices)

    nbr_local, edge_count, tile_nbrs, packed = lax.optimization_barrier(
        (nbr_local, edge_count, tile_nbrs, packed)
    )
    rows, columns = build_blocks(nbr_local, edge_count)
    owners = tile_nbrs // tile_count
    within = tile_nbrs % tile_count
    remote = owners != position
    onehot = (
        (owners.reshape(-1)[:, None] == jnp.arange(devices, dtype=jnp.int32)[None, :])
        & remote.reshape(-1)[:, None]
    ).astype(jnp.int32)
    ranking = jnp.sum((jnp.cumsum(onehot, axis=0) - onehot) * onehot, axis=1).reshape(owners.shape)
    buffer_slot = jnp.where(remote, owners * capacity + ranking, slots)
    rows_index = jnp.where(remote, tile_count + buffer_slot, within)
    held = (buffer_slot.reshape(-1)[None, :] == jnp.arange(slots, dtype=jnp.int32)[:, None]).astype(jnp.int32)
    source = jnp.sum(held * jnp.arange(NB * tile_count, dtype=jnp.int32)[None, :], axis=1)
    term_tile = source % tile_count
    term_slot = source // tile_count
    sent = columns.reshape(NB * tile_count, TILE, TILE)[term_tile * NB + term_slot]

    out, aggregated, preact_grad, gradient, terms = middle(
        rows_index, term_tile, rows, sent, x_tiles, arrived, weight,
        bias_vector.reshape(1, C), cot_tiles, devices,
    )
    returned = exchange(terms, devices)
    aggregated, preact_grad, gradient, terms = lax.optimization_barrier(
        (aggregated, preact_grad, gradient, terms)
    )
    preact_grad = preact_grad.reshape(-1, C)
    weight_part = lax.dot_general(
        aggregated.reshape(-1, C), preact_grad, (((0,), (0,)), ((), ())), preferred_element_type=jnp.float32
    )
    bias_part = jnp.sum(preact_grad.astype(jnp.float32), axis=0)
    part = jnp.concatenate([weight_part, jnp.broadcast_to(bias_part[None], (C // 2, C))])
    local = local_terms(rows_index, columns, gradient)
    summed = group_sum(part, devices, position, lambda got: lax.optimization_barrier((got, local))[0])
    normalizer = 1.0 / math.sqrt(features.shape[0] * devices)
    summed = summed * normalizer
    grad_features = final_sum(wanted, local, returned, devices)
    return (out.reshape(-1, C), grad_features.reshape(-1, C), summed[:C], summed[C])


def solution(mesh):
    return jax.shard_map(
        shards,
        mesh=mesh,
        in_specs=(
            P(("slab", "coarse", "fine"), None),
            P(),
            P(),
            P(None, ("slab", "coarse", "fine")),
            P(None, ("slab", "coarse", "fine")),
            P(None, ("slab", "coarse", "fine")),
            P(("slab", "coarse", "fine"), None),
        ),
        out_specs=(
            P(("slab", "coarse", "fine"), None),
            P(("slab", "coarse", "fine"), None),
            P("slab", None),
            P("slab"),
        ),
        check_vma=False,
    )
```

```python
import math

import jax
import jax.numpy as jnp
from jax import lax
from jax.experimental import pallas as pl
from jax.experimental.pallas import tpu as pltpu
from jax.sharding import PartitionSpec as P

C = 256
TILE = 128
NB = 4
GROUP = ("coarse", "fine")
VMEM = pltpu.MemorySpace.VMEM
SMEM = pltpu.MemorySpace.SMEM
HBM = pltpu.MemorySpace.HBM
PIECE = 32
MIDDLE_VMEM = 32 << 20


def whole(space=VMEM):
    return pl.BlockSpec(memory_space=space)


def pack_kernel(position_ref, table_ref, x_ref, packed_ref, wanted_ref, x_held, wanted_s, x_sem, table_sem, sems):
    devices, slot_count = table_ref.shape
    tile_count = x_ref.shape[0]
    capacity = packed_ref.shape[0] // devices
    load = pltpu.make_async_copy(x_ref, x_held, x_sem)
    load.start()
    position = position_ref[0]
    within = table_ref[...] - position * tile_count
    asker = lax.broadcasted_iota(jnp.int32, within.shape, 0)
    mine = (within >= 0) & (within < tile_count) & (asker != position)
    ones = jnp.where(mine, 1.0, 0.0)
    earlier = lax.broadcasted_iota(jnp.int32, (slot_count, slot_count), 0)
    later = lax.broadcasted_iota(jnp.int32, (slot_count, slot_count), 1)
    before = jnp.where(earlier < later, 1.0, 0.0).astype(jnp.bfloat16)
    ranking = jnp.dot(ones.astype(jnp.bfloat16), before, preferred_element_type=jnp.float32)
    lane = lax.broadcasted_iota(jnp.int32, wanted_ref.shape, 1)
    wanted = jnp.full(wanted_ref.shape, -1, jnp.int32)
    for rank in range(capacity):
        chosen = jnp.where(mine & (ranking.astype(jnp.int32) == rank), within + 1, 0)
        found = jnp.sum(chosen.astype(jnp.float32), axis=1, keepdims=True).astype(jnp.int32) - 1
        wanted = jnp.where(lane == rank, found, wanted)
    wanted_ref[...] = wanted
    copy = pltpu.make_async_copy(wanted_ref, wanted_s, table_sem)
    copy.start()
    copy.wait()
    load.wait()

    def each(act):
        def step(device, carry):
            for rank in range(capacity):
                tile = wanted_s[device, rank]

                @pl.when(tile >= 0)
                def _():
                    slot = device * capacity + rank
                    act(pltpu.make_async_copy(x_held.at[tile], packed_ref.at[slot], sems.at[slot]))

            return carry

        lax.fori_loop(0, devices, step, 0)

    each(lambda copy: copy.start())
    each(lambda copy: copy.wait())


def pack(position, table, x_tiles, capacity):
    devices = table.shape[0]
    return pl.pallas_call(
        pack_kernel,
        name="pack",
        in_specs=[whole(SMEM), whole(), whole(HBM)],
        out_specs=[whole(HBM), whole()],
        out_shape=[
            jax.ShapeDtypeStruct((devices * capacity, TILE, C), jnp.bfloat16),
            jax.ShapeDtypeStruct((devices, 128), jnp.int32),
        ],
        scratch_shapes=[
            pltpu.VMEM(x_tiles.shape, jnp.bfloat16),
            pltpu.SMEM((devices, 128), jnp.int32),
            pltpu.SemaphoreType.DMA,
            pltpu.SemaphoreType.DMA,
            pltpu.SemaphoreType.DMA((devices * capacity,)),
        ],
        compiler_params=pltpu.CompilerParams(vmem_limit_bytes=16 << 20),
    )(position, table, x_tiles)


def blocks_kernel(nbr_ref, count_ref, rows_ref, columns_ref):
    counts = count_ref[...].astype(jnp.float32)
    weights = counts / jnp.sum(counts, axis=0, keepdims=True)
    targets = nbr_ref[...]
    for slot in range(NB):
        local = lax.broadcasted_iota(jnp.int32, (TILE, TILE), 0) + slot * TILE
        total = jnp.zeros((TILE, TILE), jnp.float32)
        for k in range(targets.shape[0]):
            total += jnp.where(targets[k : k + 1] == local, weights[k : k + 1], 0.0)
        columns_ref[0, slot] = total.astype(jnp.bfloat16)
        rows_ref[0, :, slot * TILE : (slot + 1) * TILE] = total.T.astype(jnp.bfloat16)


def build_blocks(nbr, count):
    entries, points = nbr.shape
    tile_count = points // TILE
    return pl.pallas_call(
        blocks_kernel,
        name="blocks",
        grid=(tile_count,),
        in_specs=[pl.BlockSpec((entries, TILE), lambda t: (0, t))] * 2,
        out_specs=[
            pl.BlockSpec((1, TILE, NB * TILE), lambda t: (t, 0, 0)),
            pl.BlockSpec((1, NB, TILE, TILE), lambda t: (t, 0, 0, 0)),
        ],
        out_shape=[
            jax.ShapeDtypeStruct((tile_count, TILE, NB * TILE), jnp.bfloat16),
            jax.ShapeDtypeStruct((tile_count, NB, TILE, TILE), jnp.bfloat16),
        ],
        compiler_params=pltpu.CompilerParams(vmem_limit_bytes=8 << 20),
    )(nbr, count)


def middle_kernel(
    rows_index, term_tile, rows_ref, sent_ref, x_ref, arrived_ref, weight_ref, bias_ref, cot_ref,
    out_hbm, agg_hbm, pg_hbm, grad_hbm, terms_ref, near, terms, pre, out_ref, agg_ref, pg_ref, grad_ref,
    near_sems, sems, store_sems,
):
    tile_count = x_ref.shape[0]
    slots = arrived_ref.shape[0]
    group = pre.shape[0] // TILE
    others = pltpu.make_async_copy(arrived_ref, near.at[pl.ds(tile_count, slots)], near_sems.at[1])
    others.start()
    own = pltpu.make_async_copy(x_ref, near.at[pl.ds(0, tile_count)], near_sems.at[0])
    own.start()
    own.wait()
    others.wait()
    weight = weight_ref[...]
    bias = bias_ref[...]
    results = ((out_ref, out_hbm), (agg_ref, agg_hbm), (pg_ref, pg_hbm), (grad_ref, grad_hbm))

    def stores(step):
        part = pl.ds(step * group, group)
        return [
            pltpu.make_async_copy(held.at[part], target.at[part], store_sems.at[which, step])
            for which, (held, target) in enumerate(results)
        ]

    def group_step(step, carry):
        start = step * group
        for at in range(group):
            t = start + at
            rows = rows_ref[t]
            first = jnp.concatenate([near[t], near[rows_index[1, t]]], axis=0)
            second = jnp.concatenate([near[rows_index[2, t]], near[rows_index[3, t]]], axis=0)
            total = jnp.dot(rows[:, : 2 * TILE], first, preferred_element_type=jnp.float32)
            total += jnp.dot(rows[:, 2 * TILE :], second, preferred_element_type=jnp.float32)
            agg_ref[t] = total.astype(jnp.bfloat16)
        aggregated = agg_ref[pl.ds(start, group)].reshape(group * TILE, C)
        pre[...] = jnp.dot(aggregated, weight, preferred_element_type=jnp.float32) + bias
        for piece in range(group * TILE // PIECE):
            t = start + piece * PIECE // TILE
            part = pl.ds(piece * PIECE % TILE, PIECE)
            preact = pre[piece * PIECE : (piece + 1) * PIECE]
            sigma = jax.nn.sigmoid(preact)
            out_ref[t, part] = (preact * sigma).astype(jnp.bfloat16)
            slope = sigma * (1.0 + preact * (1.0 - sigma))
            pg_ref[t, part] = (cot_ref[t, part].astype(jnp.float32) * slope).astype(jnp.bfloat16)
        preact_grad = pg_ref[pl.ds(start, group)].reshape(group * TILE, C)
        gradient = lax.dot_general(
            preact_grad, weight, (((1,), (1,)), ((), ())), preferred_element_type=jnp.float32
        )
        grad_ref[pl.ds(start, group)] = gradient.astype(jnp.bfloat16).reshape(group, TILE, C)
        for store in stores(step):
            store.start()
        return carry

    lax.fori_loop(0, tile_count // group, group_step, 0)

    per = slots // sems.shape[0]

    def term_step(device, carry):
        for rank in range(per):
            slot = device * per + rank
            terms[slot] = jnp.dot(
                sent_ref[slot], grad_ref[term_tile[slot]], preferred_element_type=jnp.float32
            ).astype(jnp.bfloat16)
        part = pl.ds(device * per, per)
        pltpu.make_async_copy(terms.at[part], terms_ref.at[part], sems.at[device]).start()
        return carry

    lax.fori_loop(0, sems.shape[0], term_step, 0)

    def finish(device, carry):
        part = pl.ds(device * per, per)
        pltpu.make_async_copy(terms.at[part], terms_ref.at[part], sems.at[device]).wait()
        return carry

    lax.fori_loop(0, sems.shape[0], finish, 0)
    for step in range(tile_count // group):
        for store in stores(step):
            store.wait()


def middle(rows_index, term_tile, rows, sent, x_tiles, arrived, weight, bias, cot, devices):
    tile_count = x_tiles.shape[0]
    slots = arrived.shape[0]
    group = math.gcd(tile_count, 8)
    tiles = jax.ShapeDtypeStruct((tile_count, TILE, C), jnp.bfloat16)
    return pl.pallas_call(
        middle_kernel,
        name="middle",
        in_specs=[whole(SMEM)] * 2 + [whole()] * 3 + [whole(HBM)] + [whole()] * 3,
        out_specs=[whole(HBM)] * 5,
        out_shape=[tiles] * 4 + [jax.ShapeDtypeStruct((slots, TILE, C), jnp.bfloat16)],
        scratch_shapes=[
            pltpu.VMEM((tile_count + slots, TILE, C), jnp.bfloat16),
            pltpu.VMEM((slots, TILE, C), jnp.bfloat16),
            pltpu.VMEM((group * TILE, C), jnp.float32),
            *[pltpu.VMEM(tiles.shape, tiles.dtype) for _ in range(4)],
            pltpu.SemaphoreType.DMA((2,)),
            pltpu.SemaphoreType.DMA((devices,)),
            pltpu.SemaphoreType.DMA((4, tile_count // group)),
        ],
        compiler_params=pltpu.CompilerParams(vmem_limit_bytes=MIDDLE_VMEM),
    )(rows_index, term_tile, rows, sent, x_tiles, arrived, weight, bias, cot)


def local_kernel(target_ref, columns_ref, grad_ref, total_ref):
    tile_count = grad_ref.shape[0]

    def own_step(t, carry):
        total_ref[t] = jnp.dot(columns_ref[t, 0], grad_ref[t], preferred_element_type=jnp.float32)
        return carry

    lax.fori_loop(0, tile_count, own_step, 0)

    def other_step(t, carry):
        for slot in range(1, NB):
            target = target_ref[slot, t]

            @pl.when(target < tile_count)
            def _():
                total_ref[target] += jnp.dot(
                    columns_ref[t, slot], grad_ref[t], preferred_element_type=jnp.float32
                )

        return carry

    lax.fori_loop(0, tile_count, other_step, 0)


def local_terms(rows_index, columns, grad):
    return pl.pallas_call(
        local_kernel,
        name="local_terms",
        in_specs=[whole(SMEM), whole(), whole()],
        out_specs=whole(),
        out_shape=jax.ShapeDtypeStruct(grad.shape, jnp.float32),
        compiler_params=pltpu.CompilerParams(vmem_limit_bytes=24 << 20),
    )(rows_index, columns, grad)


def final_kernel(wanted_ref, local_ref, returned_ref, out_ref, total, returned, total_sem, sems):
    tile_count = local_ref.shape[0]
    devices = sems.shape[0]
    per = returned_ref.shape[0] // devices
    first = pltpu.make_async_copy(local_ref, total, total_sem)
    first.start()
    copies = []
    for device in range(devices):
        part = pl.ds(device * per, per)
        copies.append(pltpu.make_async_copy(returned_ref.at[part], returned.at[part], sems.at[device]))
        copies[-1].start()
    first.wait()
    for device in range(devices):
        copies[device].wait()
        for rank in range(per):
            target = wanted_ref[device, rank]

            @pl.when(target >= 0)
            def _():
                total[target] += returned[device * per + rank].astype(jnp.float32)

    def round_step(t, carry):
        out_ref[t] = total[t].astype(jnp.bfloat16)
        return carry

    lax.fori_loop(0, tile_count, round_step, 0)


def final_sum(wanted, local, returned, devices):
    return pl.pallas_call(
        final_kernel,
        name="final_sum",
        in_specs=[whole(SMEM), pl.BlockSpec(memory_space=pl.ANY), pl.BlockSpec(memory_space=pl.ANY)],
        out_specs=whole(),
        out_shape=jax.ShapeDtypeStruct(local.shape, jnp.bfloat16),
        scratch_shapes=[
            pltpu.VMEM(local.shape, jnp.float32),
            pltpu.VMEM(returned.shape, jnp.bfloat16),
            pltpu.SemaphoreType.DMA,
            pltpu.SemaphoreType.DMA((devices,)),
        ],
        compiler_params=pltpu.CompilerParams(vmem_limit_bytes=24 << 20),
    )(wanted, local, returned)


def exchange(array, devices):
    parted = array.reshape((devices, array.shape[0] // devices) + array.shape[1:])
    return lax.all_to_all(parted, GROUP, split_axis=0, concat_axis=0, tiled=True).reshape(array.shape)


def group_sum(part, devices, position, hold, hold_last):
    bits = devices.bit_length() - 1
    low = bits - 2

    def swap(piece, difference):
        return lax.ppermute(piece, GROUP, [(d, d ^ difference) for d in range(devices)])

    for bit in range(low):
        half = part.shape[0] // 2
        upper = (position >> bit) & 1 == 1
        got = swap(jnp.where(upper, part[:half], part[half:]), 1 << bit)
        kept = jnp.where(upper, part[half:], part[:half])
        if bit == low - 1:
            got = hold(got)
        part = kept + got
    quarters = part.reshape(4, part.shape[0] // 4, C)
    place = position >> low
    got = [swap(lax.dynamic_index_in_dim(quarters, place ^ r, 0, False), r << low) for r in range(1, 4)]
    part = lax.dynamic_index_in_dim(quarters, place, 0, False) + got[0] + got[1] + got[2]
    gathered = jnp.stack([part] + hold_last([swap(part, r << low) for r in range(1, 4)]))
    part = jnp.concatenate([lax.dynamic_index_in_dim(gathered, place ^ j, 0, False) for j in range(4)])
    for bit in reversed(range(low)):
        upper = (position >> bit) & 1 == 1
        other = swap(part, 1 << bit)
        part = jnp.where(upper, jnp.concatenate([other, part]), jnp.concatenate([part, other]))
    return part


def shards(features, weight, bias_vector, tile_nbrs, nbr_local, edge_count, cotangent):
    devices = lax.axis_size("coarse") * lax.axis_size("fine")
    position = lax.axis_index(GROUP)
    tile_count = features.shape[0] // TILE
    capacity = max(1, (NB - 1) * tile_count // (2 * (devices - 1)))
    slots = devices * capacity
    x_tiles = features.reshape(tile_count, TILE, C)
    cot_tiles = cotangent.reshape(tile_count, TILE, C)

    table = lax.all_to_all(
        jnp.broadcast_to(tile_nbrs.reshape(1, -1), (devices, NB * tile_count)),
        GROUP,
        split_axis=0,
        concat_axis=0,
        tiled=True,
    )
    packed, wanted = pack(position.reshape(1).astype(jnp.int32), table, x_tiles, capacity)
    arrived = exchange(packed, devices)

    nbr_local, edge_count, tile_nbrs, packed = lax.optimization_barrier(
        (nbr_local, edge_count, tile_nbrs, packed)
    )
    rows, columns = build_blocks(nbr_local, edge_count)
    owners = tile_nbrs // tile_count
    within = tile_nbrs % tile_count
    remote = owners != position
    onehot = (
        (owners.reshape(-1)[:, None] == jnp.arange(devices, dtype=jnp.int32)[None, :])
        & remote.reshape(-1)[:, None]
    ).astype(jnp.int32)
    ranking = jnp.sum((jnp.cumsum(onehot, axis=0) - onehot) * onehot, axis=1).reshape(owners.shape)
    buffer_slot = jnp.where(remote, owners * capacity + ranking, slots)
    rows_index = jnp.where(remote, tile_count + buffer_slot, within)
    held = (buffer_slot.reshape(-1)[None, :] == jnp.arange(slots, dtype=jnp.int32)[:, None]).astype(jnp.int32)
    source = jnp.sum(held * jnp.arange(NB * tile_count, dtype=jnp.int32)[None, :], axis=1)
    term_tile = source % tile_count
    term_slot = source // tile_count
    sent = columns.reshape(NB * tile_count, TILE, TILE)[term_tile * NB + term_slot]

    out, aggregated, preact_grad, gradient, terms = middle(
        rows_index, term_tile, rows, sent, x_tiles, arrived, weight,
        bias_vector.reshape(1, C), cot_tiles, devices,
    )
    returned = exchange(terms, devices)
    aggregated, preact_grad, gradient, terms = lax.optimization_barrier(
        (aggregated, preact_grad, gradient, terms)
    )
    preact_grad = preact_grad.reshape(-1, C)
    weight_part = lax.dot_general(
        aggregated.reshape(-1, C), preact_grad, (((0,), (0,)), ((), ())), preferred_element_type=jnp.float32
    )
    bias_part = jnp.sum(preact_grad.astype(jnp.float32), axis=0)
    part = jnp.concatenate([weight_part, jnp.broadcast_to(bias_part[None], (C // 2, C))])
    local = local_terms(rows_index, columns, gradient)
    grad_features = final_sum(wanted, local, returned, devices)
    summed = group_sum(
        part,
        devices,
        position,
        lambda got: lax.optimization_barrier((got, local))[0],
        lambda got: lax.optimization_barrier((got, grad_features))[0],
    )
    normalizer = 1.0 / math.sqrt(features.shape[0] * devices)
    summed = summed * normalizer
    return (out.reshape(-1, C), grad_features.reshape(-1, C), summed[:C], summed[C])


def solution(mesh):
    return jax.shard_map(
        shards,
        mesh=mesh,
        in_specs=(
            P(("slab", "coarse", "fine"), None),
            P(),
            P(),
            P(None, ("slab", "coarse", "fine")),
            P(None, ("slab", "coarse", "fine")),
            P(None, ("slab", "coarse", "fine")),
            P(("slab", "coarse", "fine"), None),
        ),
        out_specs=(
            P(("slab", "coarse", "fine"), None),
            P(("slab", "coarse", "fine"), None),
            P("slab", None),
            P("slab"),
        ),
        check_vma=False,
    )
```

```python
import math

import jax
import jax.numpy as jnp
from jax import lax
from jax.experimental import pallas as pl
from jax.experimental.pallas import tpu as pltpu
from jax.sharding import PartitionSpec as P

C = 256
TILE = 128
NB = 4
GROUP = ("coarse", "fine")
VMEM = pltpu.MemorySpace.VMEM
SMEM = pltpu.MemorySpace.SMEM
HBM = pltpu.MemorySpace.HBM
PIECE = 32
MIDDLE_VMEM = 32 << 20


def whole(space=VMEM):
    return pl.BlockSpec(memory_space=space)


def pack_kernel(position_ref, table_ref, x_ref, packed_ref, wanted_ref, x_held, wanted_s, x_sem, table_sem, sems):
    devices, slot_count = table_ref.shape
    tile_count = x_ref.shape[0]
    capacity = packed_ref.shape[0] // devices
    load = pltpu.make_async_copy(x_ref, x_held, x_sem)
    load.start()
    position = position_ref[0]
    within = table_ref[...] - position * tile_count
    asker = lax.broadcasted_iota(jnp.int32, within.shape, 0)
    mine = (within >= 0) & (within < tile_count) & (asker != position)
    ones = jnp.where(mine, 1.0, 0.0)
    earlier = lax.broadcasted_iota(jnp.int32, (slot_count, slot_count), 0)
    later = lax.broadcasted_iota(jnp.int32, (slot_count, slot_count), 1)
    before = jnp.where(earlier < later, 1.0, 0.0).astype(jnp.bfloat16)
    ranking = jnp.dot(ones.astype(jnp.bfloat16), before, preferred_element_type=jnp.float32)
    lane = lax.broadcasted_iota(jnp.int32, wanted_ref.shape, 1)
    wanted = jnp.full(wanted_ref.shape, -1, jnp.int32)
    for rank in range(capacity):
        chosen = jnp.where(mine & (ranking.astype(jnp.int32) == rank), within + 1, 0)
        found = jnp.sum(chosen.astype(jnp.float32), axis=1, keepdims=True).astype(jnp.int32) - 1
        wanted = jnp.where(lane == rank, found, wanted)
    wanted_ref[...] = wanted
    copy = pltpu.make_async_copy(wanted_ref, wanted_s, table_sem)
    copy.start()
    copy.wait()
    load.wait()

    def each(act):
        def step(device, carry):
            for rank in range(capacity):
                tile = wanted_s[device, rank]

                @pl.when(tile >= 0)
                def _():
                    slot = device * capacity + rank
                    act(pltpu.make_async_copy(x_held.at[tile], packed_ref.at[slot], sems.at[slot]))

            return carry

        lax.fori_loop(0, devices, step, 0)

    each(lambda copy: copy.start())
    each(lambda copy: copy.wait())


def pack(position, table, x_tiles, capacity):
    devices = table.shape[0]
    return pl.pallas_call(
        pack_kernel,
        name="pack",
        in_specs=[whole(SMEM), whole(), whole(HBM)],
        out_specs=[whole(HBM), whole()],
        out_shape=[
            HBM((devices * capacity, TILE, C), jnp.bfloat16),
            jax.ShapeDtypeStruct((devices, 128), jnp.int32),
        ],
        scratch_shapes=[
            pltpu.VMEM(x_tiles.shape, jnp.bfloat16),
            pltpu.SMEM((devices, 128), jnp.int32),
            pltpu.SemaphoreType.DMA,
            pltpu.SemaphoreType.DMA,
            pltpu.SemaphoreType.DMA((devices * capacity,)),
        ],
        compiler_params=pltpu.CompilerParams(vmem_limit_bytes=16 << 20),
    )(position, table, pltpu.with_memory_space_constraint(x_tiles, HBM))


def blocks_kernel(nbr_ref, count_ref, rows_ref, columns_ref):
    counts = count_ref[...].astype(jnp.float32)
    weights = counts / jnp.sum(counts, axis=0, keepdims=True)
    targets = nbr_ref[...]
    for slot in range(NB):
        local = lax.broadcasted_iota(jnp.int32, (TILE, TILE), 0) + slot * TILE
        total = jnp.zeros((TILE, TILE), jnp.float32)
        for k in range(targets.shape[0]):
            total += jnp.where(targets[k : k + 1] == local, weights[k : k + 1], 0.0)
        columns_ref[0, slot] = total.astype(jnp.bfloat16)
        rows_ref[0, :, slot * TILE : (slot + 1) * TILE] = total.T.astype(jnp.bfloat16)


def build_blocks(nbr, count):
    entries, points = nbr.shape
    tile_count = points // TILE
    return pl.pallas_call(
        blocks_kernel,
        name="blocks",
        grid=(tile_count,),
        in_specs=[pl.BlockSpec((entries, TILE), lambda t: (0, t))] * 2,
        out_specs=[
            pl.BlockSpec((1, TILE, NB * TILE), lambda t: (t, 0, 0)),
            pl.BlockSpec((1, NB, TILE, TILE), lambda t: (t, 0, 0, 0)),
        ],
        out_shape=[
            jax.ShapeDtypeStruct((tile_count, TILE, NB * TILE), jnp.bfloat16),
            jax.ShapeDtypeStruct((tile_count, NB, TILE, TILE), jnp.bfloat16),
        ],
        compiler_params=pltpu.CompilerParams(vmem_limit_bytes=8 << 20),
    )(nbr, count)


def middle_kernel(
    rows_index, term_tile, rows_ref, sent_ref, x_ref, arrived_ref, weight_ref, bias_ref, cot_ref,
    out_hbm, agg_hbm, pg_hbm, grad_hbm, terms_ref, near, terms, pre, out_ref, agg_ref, pg_ref, grad_ref,
    near_sems, sems, store_sems,
):
    tile_count = x_ref.shape[0]
    slots = arrived_ref.shape[0]
    group = pre.shape[0] // TILE
    others = pltpu.make_async_copy(arrived_ref, near.at[pl.ds(tile_count, slots)], near_sems.at[1])
    others.start()
    own = pltpu.make_async_copy(x_ref, near.at[pl.ds(0, tile_count)], near_sems.at[0])
    own.start()
    own.wait()
    others.wait()
    weight = weight_ref[...]
    bias = bias_ref[...]
    results = ((out_ref, out_hbm), (agg_ref, agg_hbm), (pg_ref, pg_hbm), (grad_ref, grad_hbm))

    def stores(step):
        part = pl.ds(step * group, group)
        return [
            pltpu.make_async_copy(held.at[part], target.at[part], store_sems.at[which, step])
            for which, (held, target) in enumerate(results)
        ]

    def group_step(step, carry):
        start = step * group
        for at in range(group):
            t = start + at
            rows = rows_ref[t]
            first = jnp.concatenate([near[t], near[rows_index[1, t]]], axis=0)
            second = jnp.concatenate([near[rows_index[2, t]], near[rows_index[3, t]]], axis=0)
            total = jnp.dot(rows[:, : 2 * TILE], first, preferred_element_type=jnp.float32)
            total += jnp.dot(rows[:, 2 * TILE :], second, preferred_element_type=jnp.float32)
            agg_ref[t] = total.astype(jnp.bfloat16)
        aggregated = agg_ref[pl.ds(start, group)].reshape(group * TILE, C)
        pre[...] = jnp.dot(aggregated, weight, preferred_element_type=jnp.float32) + bias
        for piece in range(group * TILE // PIECE):
            t = start + piece * PIECE // TILE
            part = pl.ds(piece * PIECE % TILE, PIECE)
            preact = pre[piece * PIECE : (piece + 1) * PIECE]
            sigma = jax.nn.sigmoid(preact)
            out_ref[t, part] = (preact * sigma).astype(jnp.bfloat16)
            slope = sigma * (1.0 + preact * (1.0 - sigma))
            pg_ref[t, part] = (cot_ref[t, part].astype(jnp.float32) * slope).astype(jnp.bfloat16)
        preact_grad = pg_ref[pl.ds(start, group)].reshape(group * TILE, C)
        gradient = lax.dot_general(
            preact_grad, weight, (((1,), (1,)), ((), ())), preferred_element_type=jnp.float32
        )
        grad_ref[pl.ds(start, group)] = gradient.astype(jnp.bfloat16).reshape(group, TILE, C)
        for store in stores(step):
            store.start()
        return carry

    lax.fori_loop(0, tile_count // group, group_step, 0)

    per = slots // sems.shape[0]

    def term_step(device, carry):
        for rank in range(per):
            slot = device * per + rank
            terms[slot] = jnp.dot(
                sent_ref[slot], grad_ref[term_tile[slot]], preferred_element_type=jnp.float32
            ).astype(jnp.bfloat16)
        part = pl.ds(device * per, per)
        pltpu.make_async_copy(terms.at[part], terms_ref.at[part], sems.at[device]).start()
        return carry

    lax.fori_loop(0, sems.shape[0], term_step, 0)

    def finish(device, carry):
        part = pl.ds(device * per, per)
        pltpu.make_async_copy(terms.at[part], terms_ref.at[part], sems.at[device]).wait()
        return carry

    lax.fori_loop(0, sems.shape[0], finish, 0)
    for step in range(tile_count // group):
        for store in stores(step):
            store.wait()


def middle(rows_index, term_tile, rows, sent, x_tiles, arrived, weight, bias, cot, devices):
    tile_count = x_tiles.shape[0]
    slots = arrived.shape[0]
    group = math.gcd(tile_count, 8)
    tiles = HBM((tile_count, TILE, C), jnp.bfloat16)
    return pl.pallas_call(
        middle_kernel,
        name="middle",
        in_specs=[whole(SMEM)] * 2 + [whole()] * 3 + [whole(HBM)] + [whole()] * 3,
        out_specs=[whole(HBM)] * 5,
        out_shape=[tiles] * 4 + [HBM((slots, TILE, C), jnp.bfloat16)],
        scratch_shapes=[
            pltpu.VMEM((tile_count + slots, TILE, C), jnp.bfloat16),
            pltpu.VMEM((slots, TILE, C), jnp.bfloat16),
            pltpu.VMEM((group * TILE, C), jnp.float32),
            *[pltpu.VMEM(tiles.shape, tiles.dtype) for _ in range(4)],
            pltpu.SemaphoreType.DMA((2,)),
            pltpu.SemaphoreType.DMA((devices,)),
            pltpu.SemaphoreType.DMA((4, tile_count // group)),
        ],
        compiler_params=pltpu.CompilerParams(vmem_limit_bytes=MIDDLE_VMEM),
    )(rows_index, term_tile, rows, sent, x_tiles, arrived, weight, bias, cot)


def local_kernel(target_ref, columns_ref, grad_ref, total_ref):
    tile_count = grad_ref.shape[0]

    def own_step(t, carry):
        total_ref[t] = jnp.dot(columns_ref[t, 0], grad_ref[t], preferred_element_type=jnp.float32)
        return carry

    lax.fori_loop(0, tile_count, own_step, 0)

    def other_step(t, carry):
        for slot in range(1, NB):
            target = target_ref[slot, t]

            @pl.when(target < tile_count)
            def _():
                total_ref[target] += jnp.dot(
                    columns_ref[t, slot], grad_ref[t], preferred_element_type=jnp.float32
                )

        return carry

    lax.fori_loop(0, tile_count, other_step, 0)


def local_terms(rows_index, columns, grad):
    return pl.pallas_call(
        local_kernel,
        name="local_terms",
        in_specs=[whole(SMEM), whole(), whole()],
        out_specs=whole(),
        out_shape=HBM(grad.shape, jnp.float32),
        compiler_params=pltpu.CompilerParams(vmem_limit_bytes=24 << 20),
    )(rows_index, columns, grad)


def final_kernel(wanted_ref, local_ref, returned_ref, out_ref, total, returned, total_sem, sems):
    tile_count = local_ref.shape[0]
    devices = sems.shape[0]
    per = returned_ref.shape[0] // devices
    first = pltpu.make_async_copy(local_ref, total, total_sem)
    first.start()
    copies = []
    for device in range(devices):
        part = pl.ds(device * per, per)
        copies.append(pltpu.make_async_copy(returned_ref.at[part], returned.at[part], sems.at[device]))
        copies[-1].start()
    first.wait()
    for device in range(devices):
        copies[device].wait()
        for rank in range(per):
            target = wanted_ref[device, rank]

            @pl.when(target >= 0)
            def _():
                total[target] += returned[device * per + rank].astype(jnp.float32)

    def round_step(t, carry):
        out_ref[t] = total[t].astype(jnp.bfloat16)
        return carry

    lax.fori_loop(0, tile_count, round_step, 0)


def final_sum(wanted, local, returned, devices):
    return pl.pallas_call(
        final_kernel,
        name="final_sum",
        in_specs=[whole(SMEM), pl.BlockSpec(memory_space=pl.ANY), pl.BlockSpec(memory_space=pl.ANY)],
        out_specs=whole(),
        out_shape=jax.ShapeDtypeStruct(local.shape, jnp.bfloat16),
        scratch_shapes=[
            pltpu.VMEM(local.shape, jnp.float32),
            pltpu.VMEM(returned.shape, jnp.bfloat16),
            pltpu.SemaphoreType.DMA,
            pltpu.SemaphoreType.DMA((devices,)),
        ],
        compiler_params=pltpu.CompilerParams(vmem_limit_bytes=24 << 20),
    )(wanted, pltpu.with_memory_space_constraint(local, HBM), returned)


def exchange(array, devices):
    parted = array.reshape((devices, array.shape[0] // devices) + array.shape[1:])
    return lax.all_to_all(parted, GROUP, split_axis=0, concat_axis=0, tiled=True).reshape(array.shape)


def group_sum(part, devices, position, hold, hold_last):
    bits = devices.bit_length() - 1
    low = bits - 2

    def swap(piece, difference):
        return lax.ppermute(piece, GROUP, [(d, d ^ difference) for d in range(devices)])

    for bit in range(low):
        half = part.shape[0] // 2
        upper = (position >> bit) & 1 == 1
        got = swap(jnp.where(upper, part[:half], part[half:]), 1 << bit)
        kept = jnp.where(upper, part[half:], part[:half])
        if bit == low - 1:
            got = hold(got)
        part = kept + got
    quarters = part.reshape(4, part.shape[0] // 4, C)
    place = position >> low
    got = [swap(lax.dynamic_index_in_dim(quarters, place ^ r, 0, False), r << low) for r in range(1, 4)]
    part = lax.dynamic_index_in_dim(quarters, place, 0, False) + got[0] + got[1] + got[2]
    gathered = jnp.stack([part] + hold_last([swap(part, r << low) for r in range(1, 4)]))
    part = jnp.concatenate([lax.dynamic_index_in_dim(gathered, place ^ j, 0, False) for j in range(4)])
    for bit in reversed(range(low)):
        upper = (position >> bit) & 1 == 1
        other = swap(part, 1 << bit)
        part = jnp.where(upper, jnp.concatenate([other, part]), jnp.concatenate([part, other]))
    return part


def shards(features, weight, bias_vector, tile_nbrs, nbr_local, edge_count, cotangent):
    devices = lax.axis_size("coarse") * lax.axis_size("fine")
    position = lax.axis_index(GROUP)
    tile_count = features.shape[0] // TILE
    capacity = max(1, (NB - 1) * tile_count // (2 * (devices - 1)))
    slots = devices * capacity
    x_tiles = features.reshape(tile_count, TILE, C)
    cot_tiles = cotangent.reshape(tile_count, TILE, C)

    table = lax.all_to_all(
        jnp.broadcast_to(tile_nbrs.reshape(1, -1), (devices, NB * tile_count)),
        GROUP,
        split_axis=0,
        concat_axis=0,
        tiled=True,
    )
    packed, wanted = pack(position.reshape(1).astype(jnp.int32), table, x_tiles, capacity)
    arrived = exchange(packed, devices)

    nbr_local, edge_count, tile_nbrs, packed = lax.optimization_barrier(
        (nbr_local, edge_count, tile_nbrs, packed)
    )
    rows, columns = build_blocks(nbr_local, edge_count)
    owners = tile_nbrs // tile_count
    within = tile_nbrs % tile_count
    remote = owners != position
    onehot = (
        (owners.reshape(-1)[:, None] == jnp.arange(devices, dtype=jnp.int32)[None, :])
        & remote.reshape(-1)[:, None]
    ).astype(jnp.int32)
    ranking = jnp.sum((jnp.cumsum(onehot, axis=0) - onehot) * onehot, axis=1).reshape(owners.shape)
    buffer_slot = jnp.where(remote, owners * capacity + ranking, slots)
    rows_index = jnp.where(remote, tile_count + buffer_slot, within)
    held = (buffer_slot.reshape(-1)[None, :] == jnp.arange(slots, dtype=jnp.int32)[:, None]).astype(jnp.int32)
    source = jnp.sum(held * jnp.arange(NB * tile_count, dtype=jnp.int32)[None, :], axis=1)
    term_tile = source % tile_count
    term_slot = source // tile_count
    sent = columns.reshape(NB * tile_count, TILE, TILE)[term_tile * NB + term_slot]

    out, aggregated, preact_grad, gradient, terms = middle(
        rows_index, term_tile, rows, sent, x_tiles, arrived, weight,
        bias_vector.reshape(1, C), cot_tiles, devices,
    )
    returned = exchange(terms, devices)
    aggregated, preact_grad, gradient, terms = lax.optimization_barrier(
        (aggregated, preact_grad, gradient, terms)
    )
    preact_grad = preact_grad.reshape(-1, C)
    weight_part = lax.dot_general(
        aggregated.reshape(-1, C), preact_grad, (((0,), (0,)), ((), ())), preferred_element_type=jnp.float32
    )
    bias_part = jnp.sum(preact_grad.astype(jnp.float32), axis=0)
    part = jnp.concatenate([weight_part, jnp.broadcast_to(bias_part[None], (C // 2, C))])
    local = local_terms(rows_index, columns, gradient)
    grad_features = final_sum(wanted, local, returned, devices)
    summed = group_sum(
        part,
        devices,
        position,
        lambda got: lax.optimization_barrier((got, local))[0],
        lambda got: lax.optimization_barrier((got, grad_features))[0],
    )
    normalizer = 1.0 / math.sqrt(features.shape[0] * devices)
    summed = summed * normalizer
    return (out.reshape(-1, C), grad_features.reshape(-1, C), summed[:C], summed[C])


def solution(mesh):
    return jax.shard_map(
        shards,
        mesh=mesh,
        in_specs=(
            P(("slab", "coarse", "fine"), None),
            P(),
            P(),
            P(None, ("slab", "coarse", "fine")),
            P(None, ("slab", "coarse", "fine")),
            P(None, ("slab", "coarse", "fine")),
            P(("slab", "coarse", "fine"), None),
        ),
        out_specs=(
            P(("slab", "coarse", "fine"), None),
            P(("slab", "coarse", "fine"), None),
            P("slab", None),
            P("slab"),
        ),
        check_vma=False,
    )
```
